32 devices in a mesh: img: 8 (over z, y), tile: 4 (over x, core).
Axes of the slice: x: 2, y: 2, z: 4, core: 2. Of those that a mesh axis runs over, the one named last changes fastest.
Arguments:
- spins: float32 [8, 3, 16, 128, 256], P('img', None, None, 'tile'), may hold values from -4.5 to 4.5
- aniso: float32 [16, 128, 256], P(None, 'tile'), may hold values from 0.2 to 2
Outputs:
- path: float32 [8, 3, 16, 128, 256], P('img', None, None, 'tile')
The draws below stay inside these ranges and needn't reach their ends.
All inputs are finite; a program needn't handle non-finite values.
Results may differ from the reference program's by a relative error of at most 0.0003.
Values sent between devices are 32-bit elements; how exact they have to be, the bound alone decides.
A program may use at most 128 MiB of HBM per device.

```python
import math
import jax
import jax.numpy as jnp
from jax import lax

NY = 256
NZ = 16
OUTER = 2
INNER = 3
IMAGES = 8
NX = 128


def draw_spins(key, part):
    noise_key = jax.random.fold_in(key, 11)
    frac_img = jnp.arange(IMAGES, dtype=jnp.float32) / (IMAGES - 1)
    frac_cell = jnp.arange(NX, dtype=jnp.float32) / (NX - 1)
    angles = jnp.pi * frac_img
    select = jnp.arange(3)
    base_dir = jnp.where(select[None, :] == 0, jnp.sin(angles)[:, None], jnp.where(select[None, :] == 2, jnp.cos(angles)[:, None], 0.0))
    base_dir = base_dir[:, :, None, None, None]
    amplitude = 0.15 * (3.0 ** frac_img)[:, None, None, None, None] * (3.0 ** frac_cell)[None, None, None, :, None]
    shape = (IMAGES, 3, NZ, NX, NY)
    noise = jnp.clip(jax.random.normal(noise_key, shape, jnp.float32), -2.5, 2.5)
    return (base_dir + amplitude * noise).astype(jnp.float32)


def shard_levels(rng, extent, split, low, top_value):
    factor_of, own = 1.0, jax.random.fold_in(rng, 6)
    for position, parts in split:
        heights = jnp.exp(jax.random.uniform(jax.random.fold_in(own, position), (parts,), jnp.float32, low / len(split), top_value / len(split)))
        factor_of = factor_of * jnp.repeat(heights, extent[position] // parts).reshape([-1 if axis == position else 1 for axis in range(len(extent))])
    return factor_of


def setup_inputs(seed: int = 0) -> dict:
    splits = jax.random.split(jax.random.key(seed), 3)
    return {
        "spins": draw_spins(jax.random.fold_in(splits[2], 71), 0),
        "aniso": jnp.clip(jnp.exp(math.log(2.0) - 2.3025851 * jax.random.uniform(splits[1], (NZ, NX, NY), jnp.float32) ** shard_levels(splits[1], (NZ, NX, NY), ((1, 4),), -0.2, 0.2)), 0.2, 2.0),
    }


exchange_coef = 1.0
cubic_coef = 0.5
spring_coef = 20.0
step_scale = 0.25
epsilon = 1e-06

def laplace(field):
    widths = [(0, 0)] * (field.ndim - 4) + [(0, 0), (1, 1), (0, 0), (1, 1)]
    padded = jnp.pad(field, widths)
    centre = padded[..., 1:-1, 1:-1, 1:-1]
    beside_all = padded[..., 2:, 1:-1, 1:-1] + padded[..., :-2, 1:-1, 1:-1]
    beside_all = beside_all + padded[..., 1:-1, 2:, 1:-1] + padded[..., 1:-1, :-2, 1:-1]
    beside_all = beside_all + padded[..., 1:-1, 1:-1, 2:] + padded[..., 1:-1, 1:-1, :-2]
    return beside_all - 6.0 * centre

def axis_select():
    return (jnp.arange(3) == 2).astype(jnp.float32)[:, None, None, None]

def force_field(middle_ext, coefs):
    middle = middle_ext[..., 1:-1, :]
    square_norm = lax.optimization_barrier(jnp.sum(middle * middle, axis=-4, keepdims=True))
    return exchange_coef * laplace(middle_ext) + coefs * middle * axis_select() - cubic_coef * (square_norm - 1.0) * middle

def hessian_point(middle, vector, coefs):
    square_norm = lax.optimization_barrier(jnp.sum(middle * middle, axis=-4, keepdims=True))
    projected = lax.optimization_barrier(jnp.sum(middle * vector, axis=-4, keepdims=True))
    return coefs * vector * axis_select() - cubic_coef * ((square_norm - 1.0) * vector + 2.0 * middle * projected)

def pad_x(field):
    widths = [(0, 0)] * (field.ndim - 2) + [(1, 1), (0, 0)]
    return jnp.pad(field, widths)

def reference(spins, aniso):
    images = spins.shape[0]
    cell_count = float(spins.size)
    image_index = jnp.arange(images, dtype=jnp.int32)
    segment_live = (image_index < images - 1).astype(jnp.float32)
    interior = ((image_index > 0) & (image_index < images - 1)).astype(jnp.float32)
    target = image_index.astype(jnp.float32) / (images - 1)
    current = spins
    for outer_step in range(OUTER):
        after_img = jnp.concatenate([current[1:], jnp.zeros_like(current[:1])])
        before_img = jnp.concatenate([jnp.zeros_like(current[:1]), current[:-1]])

        def segment_stats(couple):
            own_img, next_img = couple
            middle = 0.5 * (own_img + next_img)
            drive_own = force_field(pad_x(middle), aniso)
            difference = next_img - own_img
            return (jnp.sum(difference * difference), jnp.sum(drive_own * drive_own))
        diff_sq, drive_sq = lax.map(segment_stats, (current, after_img))
        seg_len = segment_live * jnp.sqrt(diff_sq + epsilon)
        drive_len = segment_live * jnp.sqrt(drive_sq + epsilon)
        path_len = jnp.sum(seg_len)
        time_step = path_len / jnp.sum(drive_len)
        arc_share = jnp.concatenate([jnp.zeros((1,), jnp.float32), jnp.cumsum(seg_len)[:-1]]) / path_len
        spring_pull = spring_coef * (arc_share - target) * (images - 1) / (2.0 * path_len)

        def gradient(bundle):
            before_k, own_img, after_k, pull_k, inner_k = bundle
            middle_a = 0.5 * (before_k + own_img)
            middle_b = 0.5 * (own_img + after_k)
            res_a = (own_img - before_k) / time_step - force_field(pad_x(middle_a), aniso)
            res_b = (after_k - own_img) / time_step - force_field(pad_x(middle_b), aniso)
            adjoint = exchange_coef * laplace(pad_x(res_a + res_b))
            adjoint = adjoint + hessian_point(middle_a, res_a, aniso) + hessian_point(middle_b, res_b, aniso)
            result = res_a - res_b - 0.5 * time_step * adjoint + pull_k * (after_k - before_k)
            return result * inner_k
        for inner_step in range(INNER):
            gradients = lax.map(gradient, (before_img, current, after_img, spring_pull, interior))
            grad_scale = jnp.sqrt(jnp.sum(gradients * gradients) / cell_count + epsilon)
            current = current - step_scale * gradients / grad_scale
    return current
```

```python
import functools
import jax
import jax.numpy as jnp
from jax import lax
from jax.experimental import pallas as pl
from jax.experimental.pallas import tpu as pltpu
from jax.sharding import PartitionSpec as P

OUTER = 2
INNER = 3

cubic_coef = 0.5
spring_coef = 20.0
step_scale = 0.25
epsilon = 1e-06
RIM = 2
MESH = pl.DeviceIdType.MESH


def kernel(
    I, T, cell_count,
    x_ref, an_ref, out_ref,
    cur, snap, lapq, grad, rsum, part, ani, rims, tbuf, ibuf,
    swap_sem, edge_sem, ani_sem, nb_sem, rim_sem, tsend, trecv, isend, irecv, back_sem,
):
    W, NZ, NY = x_ref.shape[1:]
    half = W // 2
    E = half + 2 * RIM
    i = lax.axis_index("img")
    t = lax.axis_index("tile")
    parity = lax.rem(i, 2)
    pair = i // 2
    pairs = I // 2
    side = lax.rem(parity + t, 2)
    partner = i + 1 - 2 * parity
    tile_nb = t - 1 + 2 * side
    has_nb = jnp.logical_and(tile_nb >= 0, tile_nb < T)
    rows = lax.broadcasted_iota(jnp.int32, (NZ, NY), 0)
    cols = lax.broadcasted_iota(jnp.int32, (NZ, NY), 1)

    barrier = pltpu.get_barrier_semaphore()
    for d in range(1, T):
        pl.semaphore_signal(barrier, inc=1, device_id=(i, lax.rem(t + d, T)), device_id_type=MESH)
    for d in range(1, I):
        pl.semaphore_signal(barrier, inc=1, device_id=(lax.rem(i + d, I), t), device_id_type=MESH)
    pl.semaphore_wait(barrier, T - 1 + I - 1)

    def send(src, dst, sems, device):
        return pltpu.make_async_remote_copy(
            src_ref=src, dst_ref=dst, send_sem=sems.at[0], recv_sem=sems.at[1],
            device_id=device, device_id_type=MESH,
        )

    def flat_lap(v):
        zero = jnp.zeros_like(v)
        total = jnp.where(rows == 0, zero, pltpu.roll(v, 1, 0))
        total = total + jnp.where(rows == NZ - 1, zero, pltpu.roll(v, NZ - 1, 0))
        total = total + jnp.where(cols == 0, zero, pltpu.roll(v, 1, 1))
        total = total + jnp.where(cols == NY - 1, zero, pltpu.roll(v, NY - 1, 1))
        return total - 6.0 * v

    def dot3(u, v):
        return u[0] * v[0] + u[1] * v[1] + u[2] * v[2]

    def fold(acc):
        hs, hl = 8, 128
        total = None
        for r in range(0, NZ, hs):
            for c in range(0, NY, hl):
                piece = acc[r : r + hs, c : c + hl]
                total = piece if total is None else total + piece
        return total

    give = (1 - side) * (half - RIM)
    keep = side * (half - RIM)
    span = half + RIM
    swap = send(
        x_ref.at[:, pl.ds(give, span)],
        cur.at[parity, :, pl.ds(side * RIM, span)],
        swap_sem, (partner, t),
    )
    swap.start()
    ani_copy = send(
        an_ref.at[side * (W - 1)],
        ani.at[(1 - side) * (half + 1)],
        ani_sem, (i, tile_nb),
    )

    @pl.when(has_nb)
    def _():
        ani_copy.start()

    def keep_own(n, carry):
        for c in range(3):
            cur[parity, c, (1 - side) * RIM + n] = x_ref[c, keep + n]
        return carry

    lax.fori_loop(0, span, keep_own, 0)

    def keep_ani(n, carry):
        ani[(1 - side) + n] = an_ref[side * (half - 1) + n]
        return carry

    lax.fori_loop(0, half + 1, keep_ani, 0)

    swap.wait()
    edge = send(
        cur.at[:, :, pl.ds(RIM + side * (half - RIM), RIM)],
        cur.at[:, :, pl.ds((1 - side) * (half + RIM), RIM)],
        edge_sem, (i, tile_nb),
    )

    @pl.when(has_nb)
    def _():
        edge.start()
        edge.wait()
        ani_copy.wait()

    outer_rim = side * (half + RIM)

    @pl.when(jnp.logical_not(has_nb))
    def _():
        for j in range(2):
            for c in range(3):
                for n in range(RIM):
                    cur[j, c, outer_rim + n] = jnp.zeros((NZ, NY), jnp.float32)
        ani[side * (half + 1)] = jnp.zeros((NZ, NY), jnp.float32)

    def reduce_all(slot, par, payload):
        size = payload.shape[0]
        tbuf[slot, t, :size] = payload
        copies = []
        for d in range(1, T):
            copies.append(pltpu.make_async_remote_copy(
                src_ref=tbuf.at[slot, t, :size], dst_ref=tbuf.at[slot, t, :size],
                send_sem=tsend.at[d - 1], recv_sem=trecv.at[par, d - 1],
                device_id=(i, lax.rem(t + d, T)), device_id_type=MESH,
            ))
        for copy in copies:
            copy.start()
        for copy in copies:
            copy.wait_recv()
        total = tbuf[slot, 0, :size]
        for d in range(1, T):
            total = total + tbuf[slot, d, :size]
        ibuf[slot, i, :size] = total
        wide = []
        for d in range(1, I):
            wide.append(pltpu.make_async_remote_copy(
                src_ref=ibuf.at[slot, i, :size], dst_ref=ibuf.at[slot, i, :size],
                send_sem=isend.at[d - 1], recv_sem=irecv.at[par, d - 1],
                device_id=(lax.rem(i + d, I), t), device_id_type=MESH,
            ))
        for copy in wide:
            copy.start()
        for copy in wide:
            copy.wait_recv()
        for copy in copies + wide:
            copy.wait_send()

    def all_sum(v):
        return jnp.sum(jnp.sum(v, axis=0, keepdims=True), axis=1, keepdims=True)

    def outer_body(o, carry):
        up = send(cur.at[1], snap.at[o, 0], nb_sem.at[o, 0], (lax.rem(i + 2, I), t))
        down = send(cur.at[0], snap.at[o, 3], nb_sem.at[o, 1], (lax.rem(i + I - 2, I), t))
        has_up = pair < pairs - 1
        has_down = pair > 0

        @pl.when(has_up)
        def _():
            up.start()

        @pl.when(has_down)
        def _():
            down.start()

        def take(n, carry):
            for j in range(2):
                for c in range(3):
                    snap[o, j + 1, c, n] = cur[j, c, n]
            return carry

        lax.fori_loop(0, E, take, 0)

        def lap_of(slot):
            def step(n, carry):
                for c in range(3):
                    lapq[slot, c, n] = (
                        flat_lap(snap[o, slot, c, n + 1]) + snap[o, slot, c, n] + snap[o, slot, c, n + 2]
                    )
                return carry

            lax.fori_loop(0, half + 2, step, 0)

        def stats(slot):
            def step(n, accs):
                diff_acc, drive_acc = accs
                e = n + RIM
                first = [snap[o, slot, c, e] for c in range(3)]
                second = [snap[o, slot + 1, c, e] for c in range(3)]
                mid = [first[c] + second[c] for c in range(3)]
                dif = [second[c] - first[c] for c in range(3)]
                diff_acc = diff_acc + dot3(dif, dif)
                s = cubic_coef * (dot3(mid, mid) - 1.0)
                f = [lapq[slot, c, n + 1] + lapq[slot + 1, c, n + 1] - s * mid[c] for c in range(3)]
                f[2] = f[2] + ani[n + 1] * mid[2]
                drive_acc = drive_acc + dot3(f, f)
                return diff_acc, drive_acc

            zero = jnp.zeros((NZ, NY), jnp.float32)
            diff_acc, drive_acc = lax.fori_loop(0, half, step, (zero, zero))
            return 4.0 * fold(diff_acc), fold(drive_acc)

        def clear(slot):
            def step(n, carry):
                for c in range(3):
                    snap[o, slot, c, n] = jnp.zeros((NZ, NY), jnp.float32)
                return carry

            lax.fori_loop(0, E, step, 0)

        lap_of(1)
        lap_of(2)
        s0 = stats(1)

        @pl.when(has_up)
        def _():
            down.wait_recv()

        @pl.when(jnp.logical_not(has_up))
        def _():
            clear(3)

        lap_of(3)
        s1 = stats(2)
        base = o * (INNER + 1)
        reduce_all(base, lax.rem(base, 2), jnp.concatenate([s0[0], s0[1], s1[0], s1[1]], axis=0))

        @pl.when(has_down)
        def _():
            up.wait_recv()

        @pl.when(jnp.logical_not(has_down))
        def _():
            clear(0)

        lap_of(0)
        path_len = jnp.zeros((1, 1), jnp.float32)
        drive_total = jnp.zeros((1, 1), jnp.float32)
        before = [jnp.zeros((1, 1), jnp.float32) for _ in range(2)]
        for s in range(I - 1):
            p, r = s // 2, 16 * (s % 2)
            d = ibuf[base, 2 * p, r : r + 8] + ibuf[base, 2 * p + 1, r : r + 8]
            v = ibuf[base, 2 * p, r + 8 : r + 16] + ibuf[base, 2 * p + 1, r + 8 : r + 16]
            seg = jnp.sqrt(all_sum(d) + epsilon)
            path_len = path_len + seg
            drive_total = drive_total + jnp.sqrt(all_sum(v) + epsilon)
            for j in range(2):
                before[j] = before[j] + seg * (s < 2 * pair + j).astype(jnp.float32)
        tau_v = path_len / drive_total
        tau_half = (0.5 * tau_v)[0, 0]
        inv2 = (2.0 / tau_v)[0, 0]
        pulls = []
        for j in range(2):
            target = (2 * pair + j).astype(jnp.float32) / (I - 1)
            pull = spring_coef * (before[j] / path_len - target) * (I - 1) / (2.0 * path_len)
            pulls.append((2.0 * pull)[0, 0])

        @pl.when(has_up)
        def _():
            up.wait_send()

        @pl.when(has_down)
        def _():
            down.wait_send()

        def inner_body(k, carry):
            for j in range(2):
                def residual(n, carry, j=j):
                    e = n + 1
                    hp = [cur[j, c, e] for c in range(3)]
                    ha = [snap[o, j, c, e] for c in range(3)]
                    hb = [snap[o, j + 2, c, e] for c in range(3)]
                    lp = [flat_lap(hp[c]) + cur[j, c, e - 1] + cur[j, c, e + 1] for c in range(3)]
                    an = ani[n]

                    def one(other, lap_other, sign):
                        m = [hp[c] + other[c] for c in range(3)]
                        s = cubic_coef * (dot3(m, m) - 1.0)
                        f = [lp[c] + lap_other[c] - s * m[c] for c in range(3)]
                        f[2] = f[2] + an * m[2]
                        r = [(hp[c] - other[c]) * (sign * inv2) - f[c] for c in range(3)]
                        q = dot3(m, r)
                        h = [s * r[c] + m[c] * q for c in range(3)]
                        h[2] = h[2] - an * r[2]
                        return r, h

                    ra, hna = one(ha, [lapq[j, c, n] for c in range(3)], 1.0)
                    rb, hnb = one(hb, [lapq[j + 2, c, n] for c in range(3)], -1.0)
                    for c in range(3):
                        rsum[j, c, n] = ra[c] + rb[c]
                        part[j, c, n] = (
                            ra[c] - rb[c] + tau_half * (hna[c] + hnb[c]) + pulls[j] * (hb[c] - ha[c])
                        )
                    return carry

                lax.fori_loop(0, half + 2, residual, 0)

            @pl.when(jnp.logical_not(has_nb))
            def _():
                for j in range(2):
                    for c in range(3):
                        rsum[j, c, side * (half + 1)] = jnp.zeros((NZ, NY), jnp.float32)

            def gradient(n, acc, j):
                live = jnp.logical_and(2 * pair + j > 0, 2 * pair + j < I - 1)
                for c in range(3):
                    lap = flat_lap(rsum[j, c, n + 1]) + rsum[j, c, n] + rsum[j, c, n + 2]
                    g = part[j, c, n + 1] - tau_half * lap
                    g = jnp.where(live, g, 0.0)
                    grad[j, c, n] = g
                    acc = acc + g * g
                return acc

            step = o * INNER + k
            acc = jnp.zeros((NZ, NY), jnp.float32)
            for j in range(2):
                acc = lax.fori_loop(0, RIM, functools.partial(gradient, j=j), acc)
                acc = lax.fori_loop(half - RIM, half, functools.partial(gradient, j=j), acc)
            inner_copy = send(
                grad.at[:, :, pl.ds((1 - side) * (half - RIM), RIM)],
                rims.at[step, 0], rim_sem.at[lax.rem(step, 2), 0], (partner, t),
            )
            inner_copy.start()
            outer_copy = send(
                grad.at[:, :, pl.ds(side * (half - RIM), RIM)],
                rims.at[step, 1], rim_sem.at[lax.rem(step, 2), 1], (i, tile_nb),
            )

            @pl.when(has_nb)
            def _():
                outer_copy.start()

            for j in range(2):
                acc = lax.fori_loop(RIM, half - RIM, functools.partial(gradient, j=j), acc)
            slot = base + 1 + k
            reduce_all(slot, lax.rem(slot, 2), fold(acc))
            total = ibuf[slot, 0, :8]
            for d in range(1, I):
                total = total + ibuf[slot, d, :8]
            scale_v = jnp.sqrt(all_sum(total) / cell_count + epsilon)
            move = (0.5 * step_scale / scale_v)[0, 0]

            def update(n, carry):
                for j in range(2):
                    for c in range(3):
                        cur[j, c, n + RIM] = cur[j, c, n + RIM] - move * grad[j, c, n]
                return carry

            lax.fori_loop(0, half, update, 0)
            inner_copy.wait()
            inner_rim = (1 - side) * (half + RIM)
            for j in range(2):
                for c in range(3):
                    for n in range(RIM):
                        cur[j, c, inner_rim + n] = cur[j, c, inner_rim + n] - move * rims[step, 0, j, c, n]

            @pl.when(has_nb)
            def _():
                outer_copy.wait()
                for j in range(2):
                    for c in range(3):
                        for n in range(RIM):
                            cur[j, c, outer_rim + n] = cur[j, c, outer_rim + n] - move * rims[step, 1, j, c, n]

            return carry

        lax.fori_loop(0, INNER, inner_body, 0)
        return carry

    lax.fori_loop(0, OUTER, outer_body, 0)

    back = send(
        cur.at[1 - parity, :, pl.ds(RIM, half)],
        out_ref.at[:, pl.ds(side * half, half)],
        back_sem, (partner, t),
    )
    back.start()

    def place(n, carry):
        for c in range(3):
            out_ref[c, side * half + n] = cur[parity, c, RIM + n]
        return carry

    lax.fori_loop(0, half, place, 0)
    back.wait()


def body(I, T, spins, aniso):
    _, comps, nz, w, ny = spins.shape
    half = w // 2
    ext = half + 2 * RIM
    cell_count = float(I * comps * nz * w * T * ny)
    x = jnp.transpose(0.5 * spins[0], (0, 2, 1, 3))
    an = jnp.transpose(aniso, (1, 0, 2))
    slots = OUTER * (INNER + 1)
    f32 = jnp.float32
    dma = pltpu.SemaphoreType.DMA
    out = pl.pallas_call(
        functools.partial(kernel, I, T, cell_count),
        out_shape=jax.ShapeDtypeStruct((comps, w, nz, ny), f32),
        in_specs=[pl.BlockSpec(memory_space=pltpu.VMEM)] * 2,
        out_specs=pl.BlockSpec(memory_space=pltpu.VMEM),
        scratch_shapes=[
            pltpu.VMEM((2, comps, ext, nz, ny), f32),
            pltpu.VMEM((OUTER, 4, comps, ext, nz, ny), f32),
            pltpu.VMEM((4, comps, half + 2, nz, ny), f32),
            pltpu.VMEM((2, comps, half, nz, ny), f32),
            pltpu.VMEM((2, comps, half + 2, nz, ny), f32),
            pltpu.VMEM((2, comps, half + 2, nz, ny), f32),
            pltpu.VMEM((half + 2, nz, ny), f32),
            pltpu.VMEM((OUTER * INNER, 2, 2, comps, RIM, nz, ny), f32),
            pltpu.VMEM((slots, T, 32, 128), f32),
            pltpu.VMEM((slots, I, 32, 128), f32),
            dma((2,)), dma((2,)), dma((2,)), dma((OUTER, 2, 2)), dma((2, 2, 2)),
            dma((T - 1,)), dma((2, T - 1)), dma((I - 1,)), dma((2, I - 1)), dma((2,)),
        ],
        compiler_params=pltpu.CompilerParams(
            collective_id=0, has_side_effects=True, vmem_limit_bytes=48 * 1024 * 1024
        ),
    )(x, an)
    return jnp.transpose(2.0 * out, (0, 2, 1, 3))[None]


def solution(mesh):
    in_specs = (P("img", None, None, "tile", None), P(None, "tile", None))
    out_specs = P("img", None, None, "tile", None)
    fn = functools.partial(body, mesh.shape["img"], mesh.shape["tile"])
    return jax.shard_map(fn, mesh=mesh, in_specs=in_specs, out_specs=out_specs, check_vma=False)
```
